32 devices in a mesh: dp: 4 (over y, x), ctx: 8 (over z, core).
Axes of the slice: x: 2, y: 2, z: 4, core: 2. Of those that a mesh axis runs over, the one named last changes fastest.
Arguments:
- inputs: bfloat16 [4, 2048, 2048], P('dp', 'ctx'), may hold values from -6 to 6
- targets: bfloat16 [4, 2048, 2048], P('dp', 'ctx'), may hold values from -6 to 6
- valid: int32 [4, 2048], P('dp', 'ctx'), may hold values from 0 to 1, as said below
- positions: int32 [4, 2048], P('dp', 'ctx'), may hold values from 0 to 3070, as said below
- ln1_gain: bfloat16 [2048], P(('dp', 'ctx')), may hold values from 0.5 to 1.5
- w_query: bfloat16 [2048, 2048], P(('dp', 'ctx')), may hold values from -0.125 to 0.125
- w_key: bfloat16 [2048, 1024], P(('dp', 'ctx')), may hold values from -0.125 to 0.125
- w_value: bfloat16 [2048, 1024], P(('dp', 'ctx')), may hold values from -0.125 to 0.125
- w_gatelogit: bfloat16 [2048, 16], P(('dp', 'ctx')), may hold values from -0.25 to 0.25
- q_gain: bfloat16 [128], P(('dp', 'ctx')), may hold values from 0.5 to 1.5
- k_gain: bfloat16 [128], P(('dp', 'ctx')), may hold values from 0.5 to 1.5
- w_output: bfloat16 [2048, 2048], P(None, ('dp', 'ctx')), may hold values from -6 to 6
- ln2_gain: bfloat16 [2048], P(('dp', 'ctx')), may hold values from 0.25 to 2.5
- w_gate: bfloat16 [2048, 6144], P(('dp', 'ctx')), may hold values from -0.125 to 0.125
- w_up: bfloat16 [2048, 6144], P(('dp', 'ctx')), may hold values from -0.125 to 0.125
- w_down: bfloat16 [6144, 2048], P(None, ('dp', 'ctx')), may hold values from -0.078125 to 0.078125
Outputs:
- output: bfloat16 [4, 2048, 2048], P('dp', 'ctx')
- loss: float32 [], replicated
- grad_inputs: float32 [4, 2048, 2048], P('dp', 'ctx')
- grad_ln1_gain: float32 [2048], P(('dp', 'ctx'))
- grad_w_query: float32 [2048, 2048], P(('dp', 'ctx'))
- grad_w_key: float32 [2048, 1024], P(('dp', 'ctx'))
- grad_w_value: float32 [2048, 1024], P(('dp', 'ctx'))
- grad_w_gatelogit: float32 [2048, 16], P(('dp', 'ctx'))
- grad_q_gain: float32 [128], P(('dp', 'ctx'))
- grad_k_gain: float32 [128], P(('dp', 'ctx'))
- grad_w_output: float32 [2048, 2048], P(None, ('dp', 'ctx'))
- grad_ln2_gain: float32 [2048], P(('dp', 'ctx'))
- grad_w_gate: float32 [2048, 6144], P(('dp', 'ctx'))
- grad_w_up: float32 [2048, 6144], P(('dp', 'ctx'))
- grad_w_down: float32 [6144, 2048], P(None, ('dp', 'ctx'))
The draws below stay inside these ranges and needn't reach their ends.
Inputs may be any that keep to these rules, and one draw needn't show every extreme that they name: The first token of every sequence has valid = 1. Along each sequence positions start at 0 and rise by 1 or 2 from one token to the next, by 2 at exactly (2047) // 2 of the steps.
All inputs are finite; a program needn't handle non-finite values.
Results may differ from the reference program's by a relative error of at most 0.017.
Values may be sent and summed in bfloat16 or wider, within the bound.
A program may use at most 512 MiB of HBM per device.

```python
import math
import jax
import jax.numpy as jnp
from jax import lax

D = 2048
H = 16
KV = 8
HD = 128
FF = 6144
SEQ = 2048
SEQS = 4
TOKENS = 8192


def draw_valid(key, part):
    dice_rolls = jax.random.randint(key, (SEQS, SEQ), 0, 1000)
    token_place = jnp.arange(SEQ, dtype=jnp.int32)[None, :]
    flat_place = jnp.arange(SEQS, dtype=jnp.int32)[:, None] * SEQ + token_place
    threshold = 60 + 900 * flat_place // (SEQS * SEQ)
    chosen = (dice_rolls < threshold) | (token_place == 0)
    return chosen.astype(jnp.int32)


def draw_positions(key, part):
    row_keys = jax.random.split(jax.random.fold_in(key, 7), SEQS)

    def one_row(row_key):
        order = jax.random.permutation(row_key, SEQ - 1)
        strides = 1 + (order < (SEQ - 1) // 2).astype(jnp.int32)
        rising = jnp.cumsum(strides).astype(jnp.int32)
        return jnp.concatenate([jnp.zeros((1,), jnp.int32), rising])
    return jax.vmap(one_row)(row_keys)


def level_of(stream_key, dims, cuts, low, high):
    level, own = 1.0, jax.random.fold_in(stream_key, 6)
    for dim, blocks in cuts:
        heights = jnp.exp(jax.random.uniform(jax.random.fold_in(own, dim), (blocks,), jnp.float32, low / len(cuts), high / len(cuts)))
        level = level * jnp.repeat(heights, dims[dim] // blocks).reshape([-1 if axis == dim else 1 for axis in range(len(dims))])
    return level


def centred(key, shape, width, most, shards=(), held_as=jnp.bfloat16):
    values = jax.random.normal(key, shape, jnp.float32) * width
    if len(shards) > 0:
        values = level_of(key, shape, shards, -0.22, 0.18) * values
    return jnp.clip(values, min=-most, max=most).astype(held_as)


def setup_inputs(seed: int = 0) -> dict:
    streams_of = jax.random.split(jax.random.key(seed), 17)
    return {
        "inputs": centred(streams_of[0], (SEQS, SEQ, D), 1.0, 6.0, ((0, 4), (1, 8))),
        "targets": centred(streams_of[1], (SEQS, SEQ, D), 1.0, 6.0, ((0, 4), (1, 8))),
        "valid": draw_valid(jax.random.fold_in(streams_of[16], 71), 0),
        "positions": draw_positions(jax.random.fold_in(streams_of[16], 71), 0),
        "ln1_gain": jnp.clip(1.0 + 0.1 * jax.random.normal(streams_of[4], (D,), jnp.float32), 0.5, 1.5).astype(jnp.bfloat16),
        "w_query": centred(streams_of[5], (D, H * HD), D ** -0.5, 0.125, ((0, 32),)),
        "w_key": centred(streams_of[6], (D, KV * HD), D ** -0.5, 0.125, ((0, 32),)),
        "w_value": centred(streams_of[7], (D, KV * HD), D ** -0.5, 0.125, ((0, 32),)),
        "w_gatelogit": centred(streams_of[8], (D, H), (D // 4) ** -0.5, 0.25, ((0, 32),)),
        "q_gain": jnp.clip(1.0 + 0.1 * jax.random.normal(streams_of[9], (HD,), jnp.float32), 0.5, 1.5).astype(jnp.bfloat16),
        "k_gain": jnp.clip(1.0 + 0.1 * jax.random.normal(streams_of[10], (HD,), jnp.float32), 0.5, 1.5).astype(jnp.bfloat16),
        "w_output": centred(streams_of[11], (H * HD, D), 1 ** -0.5, 6.0, ((1, 32),)),
        "ln2_gain": jnp.clip(jnp.exp(math.log(2.5) - 2.3025851 * jax.random.uniform(streams_of[12], (D,), jnp.float32) ** level_of(streams_of[12], (D,), ((0, 32),), -0.2, 0.2)), 0.25, 2.5).astype(jnp.bfloat16),
        "w_gate": centred(streams_of[13], (D, FF), D ** -0.5, 0.125, ((0, 32),)),
        "w_up": centred(streams_of[14], (D, FF), D ** -0.5, 0.125, ((0, 32),)),
        "w_down": centred(streams_of[15], (FF, D), FF ** -0.5, 0.078125, ((1, 32),)),
    }


@jax.custom_vjp
def low(v):
    return lax.optimization_barrier(v.astype(jnp.bfloat16)).astype(jnp.float32)

@jax.custom_vjp
def low_back(v):
    return v

def low_keep(v):
    return (low(v), None)

def low_pass(kept, grad):
    return (grad,)

def back_keep(v):
    return (v, None)

def back_low(kept, grad):
    return (low(grad),)
low.defvjp(low_keep, low_pass)
low_back.defvjp(back_keep, back_low)
EPSILON = 1e-06
ROPE_BASE = 1000000.0
MASKED = -1e+30
HIGHEST = lax.Precision.HIGHEST

def normalize(values):
    return values * lax.rsqrt(lax.optimization_barrier(jnp.mean(values * values, axis=-1, keepdims=True)) + EPSILON)

def product(left, right):
    return jnp.dot(left, right, precision=HIGHEST, preferred_element_type=jnp.float32)

def rope_tables(places):
    half_width = HD // 2
    frequency = ROPE_BASE ** (-(jnp.arange(half_width, dtype=jnp.float32) * 2.0 / HD))
    angles = places.astype(jnp.float32)[:, None] * frequency[None, :]
    cosine = jnp.concatenate([jnp.cos(angles), jnp.cos(angles)], axis=-1)
    sine = jnp.concatenate([jnp.sin(angles), jnp.sin(angles)], axis=-1)
    return (cosine, sine)

def rotate(values):
    half_width = values.shape[-1] // 2
    return jnp.concatenate([-values[..., half_width:], values[..., :half_width]], axis=-1)

def apply_rope(heads, cosine, sine):
    return heads * cosine[:, None, :] + rotate(heads) * sine[:, None, :]

def attention(queries, keys, values):
    length = queries.shape[0]
    key_block = math.gcd(length, 512)
    groups = H // KV
    blocked = queries.reshape(length // key_block, key_block, KV, groups, HD)
    key_rows = jnp.arange(length)

    def one_block(scan_item):
        query_block, first_row = scan_item
        scores = jnp.einsum('tkgd,skd->kgts', query_block, keys, precision=HIGHEST) * HD ** (-0.5)
        scores = low_back(scores)
        causal = key_rows[None, :] <= (first_row + jnp.arange(key_block))[:, None]
        scores = jnp.where(causal, scores, MASKED)
        probs = low(jax.nn.softmax(scores, axis=-1))
        attended = jnp.einsum('kgts,skd->tkgd', probs, values, precision=HIGHEST)
        return low_back(attended.reshape(key_block, H * HD))
    starts = jnp.arange(length // key_block) * key_block
    return lax.map(jax.checkpoint(one_block), (blocked, starts)).reshape(length, H * HD)

def sequence(param_set, hidden_in, teacher, weight_rows, places):
    gain_one, w_q, w_k, w_v, w_gl, gain_q, gain_k, w_out, gain_two, w_g, w_u, w_d = param_set
    length = hidden_in.shape[0]
    cosine, sine = rope_tables(places)
    normed_in = low(normalize(hidden_in) * gain_one)
    query_raw = low_back(product(normed_in, w_q))
    key_raw = low_back(product(normed_in, w_k))
    value_raw = low_back(product(normed_in, w_v))
    gate_logit = low_back(product(normed_in, w_gl))
    queries = low(apply_rope(normalize(query_raw.reshape(length, H, HD)) * gain_q, cosine, sine))
    keys = low(apply_rope(normalize(key_raw.reshape(length, KV, HD)) * gain_k, cosine, sine))
    values = low(value_raw.reshape(length, KV, HD))
    attended = attention(queries, keys, values)
    gate_open = jax.nn.sigmoid(gate_logit)
    gated = low((attended.reshape(length, H, HD) * gate_open[:, :, None]).reshape(length, H * HD))
    middle = hidden_in + low_back(product(gated, w_out))
    normed_mid = low(normalize(middle) * gain_two)
    gate_pre = low_back(product(normed_mid, w_g))
    up_proj = low_back(product(normed_mid, w_u))
    activated = low(jax.nn.silu(gate_pre) * up_proj)
    result = middle + low_back(product(activated, w_d))
    difference = result - teacher
    return (result, jnp.sum(weight_rows * lax.optimization_barrier(jnp.mean(difference * difference, axis=-1))))

def reference(inputs, targets, valid, positions, ln1_gain, w_query, w_key, w_value, w_gatelogit, q_gain, k_gain, w_output, ln2_gain, w_gate, w_up, w_down):
    param_set = tuple((array.astype(jnp.float32) for array in (ln1_gain, w_query, w_key, w_value, w_gatelogit, q_gain, k_gain, w_output, ln2_gain, w_gate, w_up, w_down)))
    teachers = targets.astype(jnp.float32)
    weight_all = valid.astype(jnp.float32)
    per_sequence = jax.checkpoint(sequence)

    def forward(params_in, hidden_all):

        def scan_step(running, scan_item):
            hidden_in, teacher, weight_rows, places = scan_item
            result, error_sum = per_sequence(params_in, hidden_in, teacher, weight_rows, places)
            return (running + error_sum, result)
        error_total, results = lax.scan(scan_step, jnp.zeros((), jnp.float32), (hidden_all, teachers, weight_all, positions))
        return (results, error_total)
    (results, error_total), pullback = jax.vjp(forward, param_set, inputs.astype(jnp.float32))
    valid_count = jnp.sum(weight_all)
    loss = error_total / valid_count
    seed_value = jnp.ones_like(error_total) * (TOKENS * D / 2.0) / valid_count
    grads, grad_inputs = pullback((jnp.zeros_like(results), seed_value))
    return (results.astype(jnp.bfloat16), loss, grad_inputs, grads[0], grads[1], grads[2], grads[3], grads[4], grads[5], grads[6], grads[7], grads[8], grads[9], grads[10], grads[11])
```

```python
import functools
import math

import jax
import jax.numpy as jnp
from jax import lax
from jax.sharding import Mesh
from jax.sharding import PartitionSpec as P

H = 16
KV = 8
HD = 128


EPSILON = 1e-06
ROPE_BASE = 1000000.0
MASKED = -1e30
PLANE = ("dp", "core")
EVERY = ("dp", "z", "core")


def normalize(values):
    return values * lax.rsqrt(jnp.mean(values * values, axis=-1, keepdims=True) + EPSILON)


def norm_back(grad, values):
    factor = lax.rsqrt(jnp.mean(values * values, axis=-1, keepdims=True) + EPSILON)
    unit = values * factor
    return factor * (grad - unit * jnp.mean(grad * unit, axis=-1, keepdims=True))


def rope_tables(places):
    half_width = HD // 2
    frequency = ROPE_BASE ** (-(jnp.arange(half_width, dtype=jnp.float32) * 2.0 / HD))
    angles = places.astype(jnp.float32)[:, None] * frequency[None, :]
    cosine = jnp.concatenate([jnp.cos(angles), jnp.cos(angles)], axis=-1)
    sine = jnp.concatenate([jnp.sin(angles), jnp.sin(angles)], axis=-1)
    return (cosine, sine)


def rotate(values):
    half_width = values.shape[-1] // 2
    return jnp.concatenate([-values[..., half_width:], values[..., :half_width]], axis=-1)


def rotate_back(values):
    half_width = values.shape[-1] // 2
    return jnp.concatenate([values[..., half_width:], -values[..., :half_width]], axis=-1)


def apply_rope(heads, cosine, sine):
    return heads * cosine[:, None, :] + rotate(heads) * sine[:, None, :]


def rope_back(grad, cosine, sine):
    return grad * cosine[:, None, :] + rotate_back(grad * sine[:, None, :])


def contract_rows(left, right):
    return lax.dot_general(
        left, right, (((0,), (0,)), ((), ())), preferred_element_type=jnp.float32
    )


def contract_cols(left, right):
    return lax.dot_general(
        left, right, (((1,), (1,)), ((), ())), preferred_element_type=jnp.float32
    )


def matmul(left, right):
    return jnp.dot(left, right, preferred_element_type=jnp.float32)


def plane_gather(rows):
    return lax.all_gather(rows, PLANE, axis=0, tiled=True)


def plane_sum(partial):
    return lax.psum_scatter(partial, PLANE, scatter_dimension=0, tiled=True)


def column_swap(values):
    return lax.all_to_all(values, "z", 0, 0, tiled=True)


def block_scores(queries, keys_all, values_all, first_row, step_index, key_block):
    place = step_index * key_block
    keys_here = lax.dynamic_slice_in_dim(keys_all, place, key_block, 0)
    values_here = lax.dynamic_slice_in_dim(values_all, place, key_block, 0)
    scores = jnp.einsum(
        "tkgd,skd->kgts", queries, keys_here, preferred_element_type=jnp.float32
    ) * queries.shape[-1] ** (-0.5)
    key_rows = place + lax.iota(jnp.int32, key_block)
    query_rows = first_row + lax.iota(jnp.int32, queries.shape[0])
    causal = key_rows[None, :] <= query_rows[:, None]
    return (scores, causal, keys_here, values_here)


def attend(queries, keys_all, values_all, first_row, key_block):
    rows_here = queries.shape[0]
    blocks_needed = (first_row + rows_here + key_block - 1) // key_block
    score_shape = (queries.shape[1], queries.shape[2], rows_here)

    def statistics(step_index, carried):
        running_max, running_sum = carried
        scores, causal, keys_here, values_here = block_scores(
            queries, keys_all, values_all, first_row, step_index, key_block
        )
        scores = jnp.where(causal, scores, MASKED)
        new_max = jnp.maximum(running_max, jnp.max(scores, axis=-1))
        weights_here = jnp.where(causal, jnp.exp(scores - new_max[..., None]), 0.0)
        return (
            new_max,
            running_sum * jnp.exp(running_max - new_max) + jnp.sum(weights_here, axis=-1),
        )

    start_state = (jnp.full(score_shape, MASKED, jnp.float32), jnp.zeros(score_shape, jnp.float32))
    running_max, running_sum = lax.fori_loop(0, blocks_needed, statistics, start_state)
    log_total = running_max + jnp.log(running_sum)

    def weigh(step_index, weighted):
        scores, causal, keys_here, values_here = block_scores(
            queries, keys_all, values_all, first_row, step_index, key_block
        )
        probs = jnp.where(causal, jnp.exp(scores - log_total[..., None]), 0.0).astype(jnp.bfloat16)
        return weighted + jnp.einsum(
            "kgts,skd->tkgd", probs, values_here, preferred_element_type=jnp.float32
        )

    weighted = lax.fori_loop(0, blocks_needed, weigh, jnp.zeros(queries.shape, jnp.float32))
    return (weighted, log_total)


def attend_back(
    queries, keys_all, values_all, first_row, key_block, log_total, d_attended, row_dot
):
    rows_here = queries.shape[0]
    blocks_needed = (first_row + rows_here + key_block - 1) // key_block
    score_scale = queries.shape[-1] ** (-0.5)

    def accumulate(step_index, carried):
        d_queries, d_keys_all, d_values_all = carried
        scores, causal, keys_here, values_here = block_scores(
            queries, keys_all, values_all, first_row, step_index, key_block
        )
        probs = jnp.where(causal, jnp.exp(scores - log_total[..., None]), 0.0)
        d_probs = jnp.einsum(
            "tkgd,skd->kgts", d_attended, values_here, preferred_element_type=jnp.float32
        )
        d_scores = (probs * (d_probs - row_dot[..., None])).astype(jnp.bfloat16)
        d_queries = (
            d_queries
            + jnp.einsum("kgts,skd->tkgd", d_scores, keys_here, preferred_element_type=jnp.float32)
            * score_scale
        )
        d_keys_here = (
            jnp.einsum("kgts,tkgd->skd", d_scores, queries, preferred_element_type=jnp.float32)
            * score_scale
        )
        d_values_here = jnp.einsum(
            "kgts,tkgd->skd",
            probs.astype(jnp.bfloat16),
            d_attended,
            preferred_element_type=jnp.float32,
        )
        place = step_index * key_block
        d_keys_all = lax.dynamic_update_slice_in_dim(d_keys_all, d_keys_here, place, 0)
        d_values_all = lax.dynamic_update_slice_in_dim(d_values_all, d_values_here, place, 0)
        return (d_queries, d_keys_all, d_values_all)

    start_state = (
        jnp.zeros(queries.shape, jnp.float32),
        jnp.zeros(keys_all.shape, jnp.float32),
        jnp.zeros(values_all.shape, jnp.float32),
    )
    return lax.fori_loop(0, blocks_needed, accumulate, start_state)


def weight_gathered(
    inputs,
    targets,
    valid,
    positions,
    ln1_gain,
    w_query,
    w_key,
    w_value,
    w_gatelogit,
    q_gain,
    k_gain,
    w_output,
    ln2_gain,
    w_gate,
    w_up,
    w_down,
):
    attn_full = (
        lax.all_gather(ln1_gain, ("dp", "ctx"), axis=0, tiled=True),
        lax.all_gather(w_query, ("dp", "ctx"), axis=0, tiled=True),
        lax.all_gather(w_key, ("dp", "ctx"), axis=0, tiled=True),
        lax.all_gather(w_value, ("dp", "ctx"), axis=0, tiled=True),
        lax.all_gather(w_gatelogit, ("dp", "ctx"), axis=0, tiled=True),
        lax.all_gather(q_gain, ("dp", "ctx"), axis=0, tiled=True),
        lax.all_gather(k_gain, ("dp", "ctx"), axis=0, tiled=True),
        lax.all_gather(w_output, ("dp", "ctx"), axis=1, tiled=True),
    )
    mlp_full = (
        lax.all_gather(ln2_gain, ("dp", "ctx"), axis=0, tiled=True),
        lax.all_gather(w_gate, ("dp", "ctx"), axis=0, tiled=True),
        lax.all_gather(w_up, ("dp", "ctx"), axis=0, tiled=True),
        lax.all_gather(w_down, ("dp", "ctx"), axis=1, tiled=True),
    )
    gain_one = attn_full[0].astype(jnp.float32)
    gain_q = attn_full[5].astype(jnp.float32)
    gain_k = attn_full[6].astype(jnp.float32)
    gain_two = mlp_full[0].astype(jnp.float32)
    hidden_in = inputs[0].astype(jnp.float32)
    rows_here = hidden_in.shape[0]
    groups = H // KV
    first_row = lax.axis_index("ctx") * rows_here
    cosine, sine = rope_tables(positions[0])
    unit_in = normalize(hidden_in)
    normed_in = (unit_in * gain_one).astype(jnp.bfloat16)
    query_raw = jnp.dot(normed_in, attn_full[1], preferred_element_type=jnp.float32)
    key_raw = jnp.dot(normed_in, attn_full[2], preferred_element_type=jnp.float32)
    value_raw = jnp.dot(normed_in, attn_full[3], preferred_element_type=jnp.float32)
    gate_logit = jnp.dot(normed_in, attn_full[4], preferred_element_type=jnp.float32)
    query_heads = query_raw.reshape(rows_here, H, HD)
    key_heads = key_raw.reshape(rows_here, KV, HD)
    unit_query = normalize(query_heads)
    unit_key = normalize(key_heads)
    queries = (
        apply_rope(unit_query * gain_q, cosine, sine)
        .astype(jnp.bfloat16)
        .reshape(rows_here, KV, groups, HD)
    )
    keys_own = apply_rope(unit_key * gain_k, cosine, sine).astype(jnp.bfloat16)
    values_own = value_raw.reshape(rows_here, KV, HD).astype(jnp.bfloat16)
    keys_all, values_all = (
        lax.all_gather(keys_own, "ctx", axis=0, tiled=True),
        lax.all_gather(values_own, "ctx", axis=0, tiled=True),
    )
    key_block = math.gcd(keys_all.shape[0], 512)
    attended, log_total = attend(queries, keys_all, values_all, first_row, key_block)
    gate_open = jax.nn.sigmoid(gate_logit)
    attended_heads = attended.reshape(rows_here, H, HD)
    gated = (attended_heads * gate_open[:, :, None]).reshape(rows_here, H * HD).astype(jnp.bfloat16)
    middle = hidden_in + jnp.dot(gated, attn_full[7], preferred_element_type=jnp.float32)
    unit_mid = normalize(middle)
    normed_mid = (unit_mid * gain_two).astype(jnp.bfloat16)
    gate_pre = jnp.dot(normed_mid, mlp_full[1], preferred_element_type=jnp.float32)
    up_proj = jnp.dot(normed_mid, mlp_full[2], preferred_element_type=jnp.float32)
    sigmoid_gate = jax.nn.sigmoid(gate_pre)
    activated = (gate_pre * sigmoid_gate * up_proj).astype(jnp.bfloat16)
    result = middle + jnp.dot(activated, mlp_full[3], preferred_element_type=jnp.float32)
    teacher = targets[0].astype(jnp.float32)
    weight_rows = valid[0].astype(jnp.float32)
    difference = result - teacher
    error_local = jnp.sum(weight_rows * jnp.mean(difference * difference, axis=-1))
    error_total, valid_count = lax.psum((error_local, jnp.sum(weight_rows)), ("dp", "ctx"))
    loss = error_total / valid_count
    tokens_all = lax.axis_size("dp") * lax.axis_size("ctx") * rows_here
    d_result = weight_rows[:, None] * difference * (tokens_all / valid_count)
    attn_back = (
        lax.all_gather(ln1_gain, ("dp", "ctx"), axis=0, tiled=True),
        lax.all_gather(w_query, ("dp", "ctx"), axis=0, tiled=True),
        lax.all_gather(w_key, ("dp", "ctx"), axis=0, tiled=True),
        lax.all_gather(w_value, ("dp", "ctx"), axis=0, tiled=True),
        lax.all_gather(w_gatelogit, ("dp", "ctx"), axis=0, tiled=True),
        lax.all_gather(q_gain, ("dp", "ctx"), axis=0, tiled=True),
        lax.all_gather(k_gain, ("dp", "ctx"), axis=0, tiled=True),
        lax.all_gather(w_output, ("dp", "ctx"), axis=1, tiled=True),
    )
    mlp_back = (
        lax.all_gather(ln2_gain, ("dp", "ctx"), axis=0, tiled=True),
        lax.all_gather(w_gate, ("dp", "ctx"), axis=0, tiled=True),
        lax.all_gather(w_up, ("dp", "ctx"), axis=0, tiled=True),
        lax.all_gather(w_down, ("dp", "ctx"), axis=1, tiled=True),
    )
    d_branch = d_result.astype(jnp.bfloat16)
    d_activated = contract_cols(d_branch, mlp_back[3])
    grad_down_full = contract_rows(activated, d_branch)
    d_gate = (
        d_activated * up_proj * sigmoid_gate * (1.0 + gate_pre * (1.0 - sigmoid_gate))
    ).astype(jnp.bfloat16)
    d_up = (d_activated * gate_pre * sigmoid_gate).astype(jnp.bfloat16)
    gate_up_share = lax.psum_scatter(
        jnp.concatenate(
            [contract_rows(normed_mid, d_gate), contract_rows(normed_mid, d_up)], axis=1
        ),
        ("dp", "ctx"),
        scatter_dimension=0,
        tiled=True,
    )
    d_normed_mid = contract_cols(d_gate, mlp_back[1]) + contract_cols(d_up, mlp_back[2])
    grad_gain_two = jnp.sum(d_normed_mid * unit_mid, axis=0)
    d_middle = d_result + norm_back(d_normed_mid * mlp_back[0].astype(jnp.float32), middle)
    d_attn = d_middle.astype(jnp.bfloat16)
    d_gated = contract_cols(d_attn, attn_back[7]).reshape(rows_here, H, HD)
    grad_out_full = contract_rows(gated, d_attn)
    d_attended = (
        (d_gated * gate_open[:, :, None]).astype(jnp.bfloat16).reshape(rows_here, KV, groups, HD)
    )
    d_gate_logit = (
        jnp.sum(d_gated * attended_heads, axis=-1) * gate_open * (1.0 - gate_open)
    ).astype(jnp.bfloat16)
    row_dot = jnp.einsum("tkgd,tkgd->kgt", d_attended.astype(jnp.float32), attended)
    keys_back, values_back = (
        lax.all_gather(keys_own, "ctx", axis=0, tiled=True),
        lax.all_gather(values_own, "ctx", axis=0, tiled=True),
    )
    d_queries, d_keys_all, d_values_all = attend_back(
        queries, keys_back, values_back, first_row, key_block, log_total, d_attended, row_dot
    )
    d_keys, d_values = (
        lax.psum_scatter(
            d_keys_all.astype(jnp.bfloat16), "ctx", scatter_dimension=0, tiled=True
        ).astype(jnp.float32),
        lax.psum_scatter(
            d_values_all.astype(jnp.bfloat16), "ctx", scatter_dimension=0, tiled=True
        ).astype(jnp.float32),
    )
    d_query_rot = rope_back(d_queries.reshape(rows_here, H, HD), cosine, sine)
    grad_gain_q = jnp.sum(d_query_rot * unit_query, axis=(0, 1))
    d_query_raw = (
        norm_back(d_query_rot * attn_back[5].astype(jnp.float32), query_heads)
        .reshape(rows_here, H * HD)
        .astype(jnp.bfloat16)
    )
    d_key_rot = rope_back(d_keys, cosine, sine)
    grad_gain_k = jnp.sum(d_key_rot * unit_key, axis=(0, 1))
    d_key_raw = (
        norm_back(d_key_rot * attn_back[6].astype(jnp.float32), key_heads)
        .reshape(rows_here, KV * HD)
        .astype(jnp.bfloat16)
    )
    d_value_raw = d_values.reshape(rows_here, KV * HD).astype(jnp.bfloat16)
    d_normed_in = contract_cols(d_query_raw, attn_back[1]) + contract_cols(d_key_raw, attn_back[2])
    d_normed_in = (
        d_normed_in
        + contract_cols(d_value_raw, attn_back[3])
        + contract_cols(d_gate_logit, attn_back[4])
    )
    grad_gain_one = jnp.sum(d_normed_in * unit_in, axis=0)
    grad_inputs = d_middle + norm_back(d_normed_in * attn_back[0].astype(jnp.float32), hidden_in)
    grad_query_full = contract_rows(normed_in, d_query_raw)
    grad_key_full = contract_rows(normed_in, d_key_raw)
    grad_value_full = contract_rows(normed_in, d_value_raw)
    grad_logit_full = contract_rows(normed_in, d_gate_logit)
    grad_terms = (
        grad_gain_one,
        grad_query_full,
        grad_key_full,
        grad_value_full,
        grad_logit_full,
        grad_gain_q,
        grad_gain_k,
        grad_out_full,
        grad_gain_two,
        grad_down_full,
    )
    shares = (
        lax.psum_scatter(grad_terms[0], ("dp", "ctx"), scatter_dimension=0, tiled=True),
        lax.psum_scatter(grad_terms[1], ("dp", "ctx"), scatter_dimension=0, tiled=True),
        lax.psum_scatter(grad_terms[2], ("dp", "ctx"), scatter_dimension=0, tiled=True),
        lax.psum_scatter(grad_terms[3], ("dp", "ctx"), scatter_dimension=0, tiled=True),
        lax.psum_scatter(grad_terms[4], ("dp", "ctx"), scatter_dimension=0, tiled=True),
        lax.psum_scatter(grad_terms[5], ("dp", "ctx"), scatter_dimension=0, tiled=True),
        lax.psum_scatter(grad_terms[6], ("dp", "ctx"), scatter_dimension=0, tiled=True),
        lax.psum_scatter(grad_terms[7], ("dp", "ctx"), scatter_dimension=1, tiled=True),
        lax.psum_scatter(grad_terms[8], ("dp", "ctx"), scatter_dimension=0, tiled=True),
        lax.psum_scatter(grad_terms[9], ("dp", "ctx"), scatter_dimension=1, tiled=True),
    )
    ffn_width = w_gate.shape[1]
    return (
        result.astype(jnp.bfloat16)[None],
        loss,
        grad_inputs[None],
        shares[0],
        shares[1],
        shares[2],
        shares[3],
        shares[4],
        shares[5],
        shares[6],
        shares[7],
        shares[8],
        gate_up_share[:, :ffn_width],
        gate_up_share[:, ffn_width:],
        shares[9],
    )


def tensor_parallel(
    dp_n,
    z_n,
    inputs,
    targets,
    valid,
    positions,
    ln1_gain,
    w_query,
    w_key,
    w_value,
    w_gatelogit,
    q_gain,
    k_gain,
    w_output,
    ln2_gain,
    w_gate,
    w_up,
    w_down,
):
    plane_n = dp_n * 2
    rows_here, width = inputs.shape[1:]
    piece = ln1_gain.shape[0]
    group = KV // plane_n
    q_heads = H // plane_n
    q_cols, k_cols = q_heads * HD, group * HD
    ff_cols = w_gate.shape[1] // plane_n
    tokens = plane_n * rows_here
    plane_at = lax.axis_index("dp") * 2 + lax.axis_index("core")

    def to_inner(values):
        lead = values.shape[:-1]
        blocks = values.reshape(lead + (dp_n, z_n, 2 * piece))
        return jnp.swapaxes(blocks, -3, -2).reshape(lead + (width,))

    def to_outer(values):
        lead = values.shape[:-1]
        blocks = values.reshape(lead + (z_n, dp_n, 2 * piece))
        return jnp.swapaxes(blocks, -3, -2).reshape(lead + (width,))

    whole_parts = jnp.concatenate([positions[0], jnp.sum(valid[0])[None].astype(jnp.int32)])
    whole_all = lax.all_gather(whole_parts, EVERY, axis=0).reshape(dp_n, z_n, 2, rows_here + 1)
    valid_count = jnp.sum(whole_all[..., -1]).astype(jnp.float32)
    places = lax.dynamic_index_in_dim(whole_all, lax.axis_index("z"), 1, False)
    places = places[..., :rows_here].reshape(tokens)

    small = jnp.concatenate([ln1_gain, ln2_gain, w_gatelogit.reshape(-1), q_gain, k_gain])
    small_all = lax.all_gather(small, EVERY, axis=0)
    small_inner = jnp.swapaxes(small_all.reshape(dp_n, z_n, 2, -1), 0, 1).reshape(
        small_all.shape
    )
    gain_one = small_inner[:, :piece].reshape(width).astype(jnp.float32)
    gain_two = small_inner[:, piece : 2 * piece].reshape(width).astype(jnp.float32)
    logit_end = 2 * piece + piece * H
    w_logit = small_inner[:, 2 * piece : logit_end].reshape(width, H)
    w_logit = lax.dynamic_slice_in_dim(w_logit, plane_at * q_heads, q_heads, 1)
    head_piece = q_gain.shape[0]
    gain_q = small_all[:, logit_end : logit_end + head_piece].reshape(HD).astype(jnp.float32)
    gain_k = small_all[:, logit_end + head_piece :].reshape(HD).astype(jnp.float32)

    def by_plane(weight):
        return jnp.swapaxes(weight.reshape(piece, plane_n, -1), 0, 1)

    attn_parts = jnp.concatenate(
        [by_plane(w_query), by_plane(w_key), by_plane(w_value), by_plane(w_output.T)], axis=2
    )
    ffn_parts = jnp.concatenate([by_plane(w_gate), by_plane(w_up), by_plane(w_down.T)], axis=2)

    def assemble(parts):
        mine = lax.all_to_all(parts, PLANE, 0, 0, tiled=True)
        mine = mine.reshape(plane_n * piece, parts.shape[2])
        return lax.all_gather(mine, "z", axis=0, tiled=True)

    attn_w = assemble(attn_parts)
    ffn_w = assemble(ffn_parts)
    w_qkv = attn_w[:, : q_cols + 2 * k_cols]
    w_out_t = attn_w[:, q_cols + 2 * k_cols :]
    w_gate_up = ffn_w[:, : 2 * ff_cols]
    w_down_t = ffn_w[:, 2 * ff_cols :]

    hidden_in = to_inner(inputs[0]).astype(jnp.float32)
    unit_in = normalize(hidden_in)
    normed_in = (unit_in * gain_one).astype(jnp.bfloat16)
    normed_all = plane_gather(normed_in)
    cosine, sine = rope_tables(places)
    qkv_raw = matmul(normed_all, w_qkv)
    gate_logit = matmul(normed_all, w_logit)
    query_heads = qkv_raw[:, :q_cols].reshape(tokens, q_heads, HD)
    key_heads = qkv_raw[:, q_cols : q_cols + k_cols].reshape(tokens, group, HD)
    unit_query = normalize(query_heads)
    unit_key = normalize(key_heads)
    queries = apply_rope(unit_query * gain_q, cosine, sine).astype(jnp.bfloat16)
    keys = apply_rope(unit_key * gain_k, cosine, sine).astype(jnp.bfloat16)
    sent = jnp.concatenate(
        [
            queries.reshape(tokens, q_cols),
            keys.reshape(tokens, k_cols),
            qkv_raw[:, q_cols + k_cols :].astype(jnp.bfloat16),
        ],
        axis=1,
    )
    held = column_swap(sent)
    queries = held[:, :q_cols].reshape(tokens, group, q_heads // group, HD)
    keys = held[:, q_cols : q_cols + k_cols].reshape(tokens, group, HD)
    values = held[:, q_cols + k_cols :].reshape(tokens, group, HD)
    causal = lax.iota(jnp.int32, tokens)[None, :] <= lax.iota(jnp.int32, tokens)[:, None]
    score_scale = HD ** (-0.5)
    scores = (
        jnp.einsum("tkgd,skd->kgts", queries, keys, preferred_element_type=jnp.float32)
        * score_scale
    )
    scores = jnp.where(causal, scores, MASKED)
    log_total = jax.nn.logsumexp(scores, axis=-1)
    probs = jnp.exp(scores - log_total[..., None])
    attended = jnp.einsum(
        "kgts,skd->tkgd", probs.astype(jnp.bfloat16), values, preferred_element_type=jnp.float32
    )
    attended_back = column_swap(attended.astype(jnp.bfloat16).reshape(tokens, q_cols))
    attended_heads = attended_back.reshape(tokens, q_heads, HD).astype(jnp.float32)
    gate_open = jax.nn.sigmoid(gate_logit)
    gated = (attended_heads * gate_open[:, :, None]).reshape(tokens, q_cols).astype(jnp.bfloat16)
    branch = plane_sum(contract_cols(gated, w_out_t).astype(jnp.bfloat16))
    middle = hidden_in + branch.astype(jnp.float32)
    unit_mid = normalize(middle)
    normed_mid = plane_gather((unit_mid * gain_two).astype(jnp.bfloat16))
    gate_up = matmul(normed_mid, w_gate_up)
    gate_pre, up_proj = gate_up[:, :ff_cols], gate_up[:, ff_cols:]
    sigmoid_gate = jax.nn.sigmoid(gate_pre)
    activated = (gate_pre * sigmoid_gate * up_proj).astype(jnp.bfloat16)
    branch = plane_sum(contract_cols(activated, w_down_t).astype(jnp.bfloat16))
    result = middle + branch.astype(jnp.float32)

    weight_rows = valid[0].astype(jnp.float32)
    difference = result - to_inner(targets[0]).astype(jnp.float32)
    error_local = jnp.sum(weight_rows * jnp.mean(difference * difference, axis=-1))
    tokens_all = dp_n * z_n * 2 * rows_here
    d_result = weight_rows[:, None] * difference * (tokens_all / valid_count)
    d_branch = plane_gather(d_result.astype(jnp.bfloat16))
    d_activated = matmul(d_branch, w_down_t)
    grad_down_t = contract_rows(d_branch, activated).astype(jnp.bfloat16)
    d_gate = d_activated * up_proj * sigmoid_gate * (1.0 + gate_pre * (1.0 - sigmoid_gate))
    d_up = d_activated * gate_pre * sigmoid_gate
    d_gate_up = jnp.concatenate([d_gate, d_up], axis=1).astype(jnp.bfloat16)
    grad_gate_up = contract_rows(normed_mid, d_gate_up).astype(jnp.bfloat16)
    d_normed_mid = plane_sum(contract_cols(d_gate_up, w_gate_up).astype(jnp.bfloat16)).astype(
        jnp.float32
    )
    grad_gain_two = jnp.sum(d_normed_mid * unit_mid, axis=0)
    d_middle = d_result + norm_back(d_normed_mid * gain_two, middle)

    def settle(grads):
        summed = lax.psum_scatter(grads, "z", scatter_dimension=0, tiled=True)
        return lax.all_to_all(
            summed.reshape(plane_n, piece, grads.shape[1]), PLANE, 0, 0, tiled=True
        )

    def take(settled, start, size):
        part = jnp.swapaxes(settled[:, :, start : start + size], 0, 1)
        return part.reshape(piece, plane_n * size).astype(jnp.float32)

    gate_up_own = settle(grad_gate_up)
    down_own = settle(grad_down_t)

    d_attn = plane_gather(d_middle.astype(jnp.bfloat16))
    d_gated = matmul(d_attn, w_out_t).reshape(tokens, q_heads, HD)
    grad_out_t = contract_rows(d_attn, gated).astype(jnp.bfloat16)
    d_attended = (d_gated * gate_open[:, :, None]).astype(jnp.bfloat16)
    d_gate_logit = (
        jnp.sum(d_gated * attended_heads, axis=-1) * gate_open * (1.0 - gate_open)
    ).astype(jnp.bfloat16)
    d_attended = column_swap(d_attended.reshape(tokens, q_cols)).reshape(queries.shape)
    row_dot = jnp.einsum("tkgd,tkgd->kgt", d_attended.astype(jnp.float32), attended)
    d_probs = jnp.einsum(
        "tkgd,skd->kgts", d_attended, values, preferred_element_type=jnp.float32
    )
    d_scores = (probs * (d_probs - row_dot[..., None])).astype(jnp.bfloat16)
    d_queries = (
        jnp.einsum("kgts,skd->tkgd", d_scores, keys, preferred_element_type=jnp.float32)
        * score_scale
    )
    d_keys = (
        jnp.einsum("kgts,tkgd->skd", d_scores, queries, preferred_element_type=jnp.float32)
        * score_scale
    )
    d_values = jnp.einsum(
        "kgts,tkgd->skd",
        probs.astype(jnp.bfloat16),
        d_attended,
        preferred_element_type=jnp.float32,
    )
    sent = jnp.concatenate(
        [
            d_queries.reshape(tokens, q_cols),
            d_keys.reshape(tokens, k_cols),
            d_values.reshape(tokens, k_cols),
        ],
        axis=1,
    ).astype(jnp.bfloat16)
    held = column_swap(sent)
    d_query_rot = rope_back(
        held[:, :q_cols].reshape(tokens, q_heads, HD).astype(jnp.float32), cosine, sine
    )
    d_key_rot = rope_back(
        held[:, q_cols : q_cols + k_cols].reshape(tokens, group, HD).astype(jnp.float32),
        cosine,
        sine,
    )
    grad_gain_q = jnp.sum(d_query_rot * unit_query, axis=(0, 1))
    grad_gain_k = jnp.sum(d_key_rot * unit_key, axis=(0, 1))
    d_qkv = jnp.concatenate(
        [
            norm_back(d_query_rot * gain_q, query_heads)
            .reshape(tokens, q_cols)
            .astype(jnp.bfloat16),
            norm_back(d_key_rot * gain_k, key_heads).reshape(tokens, k_cols).astype(jnp.bfloat16),
            held[:, q_cols + k_cols :],
        ],
        axis=1,
    )
    grad_qkv = contract_rows(normed_all, d_qkv).astype(jnp.bfloat16)
    grad_logit = contract_rows(normed_all, d_gate_logit)
    attn_own = settle(jnp.concatenate([grad_qkv, grad_out_t], axis=1))
    d_normed_in = contract_cols(d_qkv, w_qkv) + contract_cols(d_gate_logit, w_logit)
    d_normed_in = plane_sum(d_normed_in.astype(jnp.bfloat16)).astype(jnp.float32)
    grad_gain_one = jnp.sum(d_normed_in * unit_in, axis=0)
    grad_inputs = d_middle + norm_back(d_normed_in * gain_one, hidden_in)

    devices = dp_n * z_n * 2
    logit_wide = lax.dynamic_update_slice(
        jnp.zeros((width, H), jnp.float32), grad_logit, (0, plane_at * q_heads)
    )

    def outer_rows(values):
        return jnp.swapaxes(values.reshape(z_n, dp_n, 2, -1), 0, 1).reshape(devices, -1)

    small_sums = jnp.concatenate(
        [
            outer_rows(grad_gain_one),
            outer_rows(grad_gain_two),
            outer_rows(logit_wide),
            grad_gain_q.reshape(devices, -1),
            grad_gain_k.reshape(devices, -1),
            jnp.full((devices, 1), error_local),
        ],
        axis=1,
    )
    small_own = lax.psum_scatter(small_sums.reshape(-1), EVERY, scatter_dimension=0, tiled=True)
    loss = small_own[-1] / valid_count
    return (
        to_outer(result.astype(jnp.bfloat16))[None],
        loss,
        to_outer(grad_inputs)[None],
        small_own[:piece],
        take(attn_own, 0, q_cols),
        take(attn_own, q_cols, k_cols),
        take(attn_own, q_cols + k_cols, k_cols),
        small_own[2 * piece : logit_end].reshape(piece, H),
        small_own[logit_end : logit_end + head_piece],
        small_own[logit_end + head_piece : -1],
        take(attn_own, q_cols + 2 * k_cols, q_cols).T,
        small_own[piece : 2 * piece],
        take(gate_up_own, 0, ff_cols),
        take(gate_up_own, ff_cols, ff_cols),
        take(down_own, 0, ff_cols).T,
    )


def solution(mesh):
    dp_n, ctx_n = mesh.shape["dp"], mesh.shape["ctx"]
    split = ctx_n == 2 * dp_n and KV % (2 * dp_n) == 0
    if split:
        mesh = Mesh(mesh.devices.reshape(dp_n, ctx_n // 2, 2), EVERY)
        on_device = functools.partial(tensor_parallel, dp_n, ctx_n // 2)
        ctx, every = ("z", "core"), EVERY
    else:
        on_device = weight_gathered
        ctx, every = "ctx", ("dp", "ctx")
    tokens, rows, cols, flat = P("dp", ctx, None), P(every, None), P(None, every), P(every)
    return jax.shard_map(
        on_device,
        mesh=mesh,
        in_specs=(
            tokens,
            tokens,
            P("dp", ctx),
            P("dp", ctx),
            flat,
            rows,
            rows,
            rows,
            rows,
            flat,
            flat,
            cols,
            flat,
            rows,
            rows,
            cols,
        ),
        out_specs=(
            tokens,
            P(),
            tokens,
            flat,
            rows,
            rows,
            rows,
            rows,
            flat,
            flat,
            cols,
            flat,
            rows,
            rows,
            cols,
        ),
        check_vma=False,
    )
```

```python
import functools
import math

import jax
import jax.numpy as jnp
from jax import lax
from jax.experimental import pallas as pl
from jax.experimental.pallas import tpu as pltpu
from jax.sharding import Mesh
from jax.sharding import PartitionSpec as P

H = 16
KV = 8
HD = 128


EPSILON = 1e-06
ROPE_BASE = 1000000.0
MASKED = -1e30
PLANE = ("dp", "core")
EVERY = ("dp", "z", "core")


def normalize(values):
    return values * lax.rsqrt(jnp.mean(values * values, axis=-1, keepdims=True) + EPSILON)


def norm_back(grad, values):
    factor = lax.rsqrt(jnp.mean(values * values, axis=-1, keepdims=True) + EPSILON)
    unit = values * factor
    return factor * (grad - unit * jnp.mean(grad * unit, axis=-1, keepdims=True))


def rope_tables(places):
    half_width = HD // 2
    frequency = ROPE_BASE ** (-(jnp.arange(half_width, dtype=jnp.float32) * 2.0 / HD))
    angles = places.astype(jnp.float32)[:, None] * frequency[None, :]
    cosine = jnp.concatenate([jnp.cos(angles), jnp.cos(angles)], axis=-1)
    sine = jnp.concatenate([jnp.sin(angles), jnp.sin(angles)], axis=-1)
    return (cosine, sine)


def rotate(values):
    half_width = values.shape[-1] // 2
    return jnp.concatenate([-values[..., half_width:], values[..., :half_width]], axis=-1)


def rotate_back(values):
    half_width = values.shape[-1] // 2
    return jnp.concatenate([values[..., half_width:], -values[..., :half_width]], axis=-1)


def apply_rope(heads, cosine, sine):
    return heads * cosine[:, None, :] + rotate(heads) * sine[:, None, :]


def rope_back(grad, cosine, sine):
    return grad * cosine[:, None, :] + rotate_back(grad * sine[:, None, :])


def contract_rows(left, right):
    return lax.dot_general(
        left, right, (((0,), (0,)), ((), ())), preferred_element_type=jnp.float32
    )


def contract_cols(left, right):
    return lax.dot_general(
        left, right, (((1,), (1,)), ((), ())), preferred_element_type=jnp.float32
    )


def matmul(left, right):
    return jnp.dot(left, right, preferred_element_type=jnp.float32)


MESH = pl.DeviceIdType.MESH
HBM = pl.BlockSpec(memory_space=pltpu.HBM)
VMEM = pl.BlockSpec(memory_space=pltpu.VMEM)
STRIP = 16
TILE = 128


def place():
    dp, z, core = lax.axis_index("dp"), lax.axis_index("z"), lax.axis_index("core")
    across = dp + 1 - 2 * lax.rem(dp, 2)
    along = dp + 2 - 4 * (dp // 2)
    return dp, z, core, across, along, across + along - dp


def meet(devices):
    barrier = pltpu.get_barrier_semaphore()
    for device in devices:
        pl.semaphore_signal(barrier, inc=1, device_id=device, device_id_type=MESH)
    pl.semaphore_wait(barrier, len(devices))


def swap_tiles(values):
    return jnp.concatenate(
        [
            values[:, TILE * (4 * (t % 4) + t // 4) : TILE * (4 * (t % 4) + t // 4 + 1)]
            for t in range(16)
        ],
        axis=1,
    )


def spread(own, out, send, recv):
    dp, z, core, across, along, corner = place()
    half = own.shape[0] // 2
    first, second = pl.ds(0, half), pl.ds(half, half)
    x_side, y_side, twin = (across, z, core), (along, z, core), (dp, z, 1 - core)
    mine, of_x, of_y, of_d = (2 * d + core for d in (dp, across, along, corner))

    def copy(index, source, slot, part, device):
        return pltpu.make_async_remote_copy(
            src_ref=source,
            dst_ref=out.at[slot, part],
            send_sem=send.at[index],
            recv_sem=recv.at[index],
            device_id=device,
            device_id_type=MESH,
        )

    copies = [
        copy(0, own.at[first], mine, first, x_side),
        copy(1, own.at[second], mine, second, x_side),
        copy(2, own.at[second], mine, second, y_side),
        copy(3, own.at[first], mine, first, y_side),
        copy(4, out.at[of_x, first], of_x, first, y_side),
        copy(5, out.at[of_y, second], of_y, second, x_side),
        copy(6, own.at[first], mine, first, twin),
        copy(7, own.at[second], mine, second, twin),
        copy(8, out.at[of_x, first], of_x, first, twin),
        copy(9, out.at[of_x, second], of_x, second, twin),
        copy(10, out.at[of_y, first], of_y, first, twin),
        copy(11, out.at[of_y, second], of_y, second, twin),
        copy(12, out.at[of_d, first], of_d, first, twin),
        copy(13, out.at[of_d, second], of_d, second, twin),
    ]

    def start_first():
        for index in (0, 3, 6):
            copies[index].start()

    def start_second():
        for index in (2, 1, 7):
            copies[index].start()

    def finish():
        for arrived, onward in ((0, (4, 8)), (2, (5, 11)), (1, (9,)), (3, (10,)), (4, (12,)), (5, (13,))):
            copies[arrived].wait_recv()
            for index in onward:
                copies[index].start()
        for index in range(6, 14):
            copies[index].wait_recv()
        for each in copies:
            each.wait_send()

    return start_first, start_second, finish


def gather_kernel(own, out, local, send, recv):
    dp, z, core, across, along, corner = place()
    meet([(across, z, core), (along, z, core), (dp, z, 1 - core)])
    keep = pltpu.make_async_copy(own, out.at[2 * dp + core], local)
    keep.start()
    start_first, start_second, finish = spread(own, out, send, recv)
    start_first()
    start_second()
    finish()
    keep.wait()


def plane_gather(rows):
    out = pl.pallas_call(
        gather_kernel,
        name="plane_gather",
        out_shape=jax.ShapeDtypeStruct((8,) + rows.shape, rows.dtype),
        in_specs=[HBM],
        out_specs=HBM,
        scratch_shapes=[
            pltpu.SemaphoreType.DMA(()),
            pltpu.SemaphoreType.DMA((14,)),
            pltpu.SemaphoreType.DMA((14,)),
        ],
        compiler_params=pltpu.CompilerParams(has_side_effects=True, collective_id=0),
        cost_estimate=pl.CostEstimate(flops=0, bytes_accessed=120 << 20, transcendentals=0),
    )(rows)
    return out.reshape(-1, rows.shape[1])


def sum_kernel(tail, gathers, n_in, n_out, *refs):
    partial, refs = refs[0], refs[1:]
    ins, outs, refs = refs[:n_in], refs[n_in : n_in + n_out], refs[n_in + n_out :]
    for out in outs:
        if out.shape[0] == STRIP:
            out[...] = jnp.zeros_like(out)
    if gathers:
        spread_out, refs = refs[0], refs[1:]
        own, refs = refs[0], refs[1:]
    held, twins, passed, load, send_a, recv_a, send_b, recv_b = refs[:8]
    dp, z, core, across, along, corner = place()
    meet([(across, z, core), (along, z, core), (dp, z, 1 - core)])
    half = partial.shape[1] // 2
    x_side, y_side, twin = (across, z, core), (along, z, core), (dp, z, 1 - core)
    owners = (dp, across, along, corner)
    order = [(3, 0), (3, 1), (1, 0), (2, 1), (2, 0), (1, 1), (0, 0), (0, 1)]
    from_twin, from_own = {}, {}
    for index, (owner, part) in enumerate(order):
        rows = pl.ds(part * half, half)
        from_twin[owner, part] = pltpu.make_async_remote_copy(
            src_ref=partial.at[2 * owners[owner] + 1 - core, rows],
            dst_ref=twins.at[owner, part],
            send_sem=send_a.at[index],
            recv_sem=recv_a.at[index],
            device_id=twin,
            device_id_type=MESH,
        )
        from_own[owner, part] = pltpu.make_async_copy(
            partial.at[2 * owners[owner] + core, rows], held.at[owner, part], load.at[index]
        )
    for key in order:
        from_twin[key].start()
        from_own[key].start()

    def arrive(owner, part):
        from_twin[owner, part].wait_recv()
        from_own[owner, part].wait()

    def add(owner, part, others):
        @pl.loop(0, half // STRIP)
        def _(step):
            rows = pl.ds(pl.multiple_of(step * STRIP, STRIP), STRIP)
            total = held[owner, part, rows].astype(jnp.float32)
            total = total + twins[owner, part, rows].astype(jnp.float32)
            for other in others:
                total = total + passed[other, rows].astype(jnp.float32)
            held[owner, part, rows] = total.astype(jnp.bfloat16)

    def last(part, others):
        @pl.loop(0, half // STRIP)
        def _(step):
            rows = pl.ds(pl.multiple_of(step * STRIP, STRIP), STRIP)
            total = held[0, part, rows].astype(jnp.float32)
            total = total + twins[0, part, rows].astype(jnp.float32)
            for other in others:
                total = total + passed[other, rows].astype(jnp.float32)
            rows = pl.ds(pl.multiple_of(part * half + step * STRIP, STRIP), STRIP)
            sent = tail(rows, total, ins, outs)
            if gathers:
                own[rows] = sent

    def pass_on(index, owner, part, device):
        copy = pltpu.make_async_remote_copy(
            src_ref=held.at[owner, part],
            dst_ref=passed.at[index],
            send_sem=send_b.at[index],
            recv_sem=recv_b.at[index],
            device_id=device,
            device_id_type=MESH,
        )
        copy.start()
        return copy

    hops = []
    for index, (owner, part, device) in enumerate(
        [(3, 0, x_side), (3, 1, y_side), (1, 0, x_side), (2, 1, y_side)]
    ):
        arrive(owner, part)
        add(owner, part, ())
        hops.append(pass_on(index, owner, part, device))
    arrive(2, 0)
    hops[0].wait_recv()
    add(2, 0, (0,))
    hops.append(pass_on(4, 2, 0, y_side))
    arrive(1, 1)
    hops[1].wait_recv()
    add(1, 1, (1,))
    hops.append(pass_on(5, 1, 1, x_side))
    arrive(0, 0)
    arrive(0, 1)
    hops[2].wait_recv()
    hops[3].wait_recv()
    if gathers:
        keep = pltpu.make_async_copy(own, spread_out.at[2 * dp + core], refs[8])
        start_first, start_second, finish = spread(own, spread_out, refs[9], refs[10])
    hops[4].wait_recv()
    last(0, (2, 4))
    if gathers:
        start_first()
    hops[5].wait_recv()
    last(1, (3, 5))
    if gathers:
        start_second()
        keep.start()
        finish()
        keep.wait()
    for key in order:
        from_twin[key].wait_send()
    for hop in hops:
        hop.wait_send()


def plane_sum(name, number, tail, partial, ins, outs, gathers):
    width = partial.shape[1]
    partial = partial.reshape(8, -1, width)
    rows = partial.shape[1]
    half = rows // 2
    out_shape = [jax.ShapeDtypeStruct(shape, dtype) for shape, dtype in outs]
    out_specs = [VMEM] * len(outs)
    scratch = [
        pltpu.VMEM((4, 2, half, width), jnp.bfloat16),
        pltpu.VMEM((4, 2, half, width), jnp.bfloat16),
        pltpu.VMEM((6, half, width), jnp.bfloat16),
        pltpu.SemaphoreType.DMA((8,)),
        pltpu.SemaphoreType.DMA((8,)),
        pltpu.SemaphoreType.DMA((8,)),
        pltpu.SemaphoreType.DMA((6,)),
        pltpu.SemaphoreType.DMA((6,)),
    ]
    if gathers:
        out_shape.append(jax.ShapeDtypeStruct((8, rows, width), jnp.bfloat16))
        out_specs.append(HBM)
        scratch = (
            [pltpu.VMEM((rows, width), jnp.bfloat16)]
            + scratch
            + [
                pltpu.SemaphoreType.DMA(()),
                pltpu.SemaphoreType.DMA((14,)),
                pltpu.SemaphoreType.DMA((14,)),
            ]
        )
    results = pl.pallas_call(
        functools.partial(sum_kernel, tail, gathers, len(ins), len(outs)),
        name=name,
        out_shape=out_shape,
        in_specs=[HBM] + [VMEM] * len(ins),
        out_specs=out_specs,
        scratch_shapes=scratch,
        compiler_params=pltpu.CompilerParams(
            has_side_effects=True, collective_id=number, vmem_limit_bytes=48 << 20
        ),
        cost_estimate=pl.CostEstimate(flops=0, bytes_accessed=240 << 20, transcendentals=0),
    )(partial, *ins)
    if gathers:
        results = list(results[:-1]) + [results[-1].reshape(-1, width)]
    return results


def middle_tail(rows, total, ins, outs):
    hidden, gain = ins
    (middle,) = outs
    mid = swap_tiles(hidden[rows]).astype(jnp.float32) + total
    middle[rows] = mid
    return (normalize(mid) * gain[...]).astype(jnp.bfloat16)


def result_tail(rows, total, ins, outs):
    middle, targets, counted, weight = ins
    result, d_result, error = outs

    value = middle[rows] + total
    result[rows] = swap_tiles(value.astype(jnp.bfloat16))
    difference = value - swap_tiles(targets[rows]).astype(jnp.float32)
    error[...] += counted[rows] * (difference * difference)
    grad = weight[rows] * difference
    d_result[rows] = grad
    return grad.astype(jnp.bfloat16)


def middle_back_tail(rows, total, ins, outs):
    middle, gain, d_result = ins
    d_middle, grad_gain = outs
    mid = middle[rows]
    factor = lax.rsqrt(jnp.mean(mid * mid, axis=-1, keepdims=True) + EPSILON)
    unit = mid * factor
    grad_gain[...] += total * unit
    grad = total * gain[...]
    back = factor * (grad - unit * jnp.mean(grad * unit, axis=-1, keepdims=True))
    back = d_result[rows] + back
    d_middle[rows] = back
    return back.astype(jnp.bfloat16)


def inputs_back_tail(rows, total, ins, outs):
    hidden, gain, d_middle = ins
    grad_inputs, grad_gain = outs
    values = swap_tiles(hidden[rows]).astype(jnp.float32)
    factor = lax.rsqrt(jnp.mean(values * values, axis=-1, keepdims=True) + EPSILON)
    unit = values * factor
    grad_gain[...] += total * unit
    grad = total * gain[...]
    back = factor * (grad - unit * jnp.mean(grad * unit, axis=-1, keepdims=True))
    grad_inputs[rows] = swap_tiles(d_middle[rows] + back)


Q_BLOCK = 256


def column_copies(sent, landed, send, recv, local):
    dp, z, core = lax.axis_index("dp"), lax.axis_index("z"), lax.axis_index("core")

    def start(to):
        @pl.when(to != z)
        def _():
            pltpu.make_async_remote_copy(
                src_ref=sent.at[to],
                dst_ref=landed.at[z],
                send_sem=send.at[to],
                recv_sem=recv.at[z],
                device_id=(dp, to, core),
                device_id_type=MESH,
            ).start()

        @pl.when(to == z)
        def _():
            pltpu.make_async_copy(sent.at[to], landed.at[to], local).start()

    def await_arrival(source):
        @pl.when(source != z)
        def _():
            pltpu.make_async_remote_copy(
                src_ref=sent.at[source],
                dst_ref=landed.at[source],
                send_sem=send.at[source],
                recv_sem=recv.at[source],
                device_id=(dp, source, core),
                device_id_type=MESH,
            ).wait_recv()

        @pl.when(source == z)
        def _():
            pltpu.make_async_copy(sent.at[source], landed.at[source], local).wait()

    def await_sent(to):
        @pl.when(to != z)
        def _():
            pltpu.make_async_remote_copy(
                src_ref=sent.at[to],
                dst_ref=landed.at[z],
                send_sem=send.at[to],
                recv_sem=recv.at[z],
                device_id=(dp, to, core),
                device_id_type=MESH,
            ).wait_send()

    return start, await_arrival, await_sent


def meet_column():
    dp, z, core = lax.axis_index("dp"), lax.axis_index("z"), lax.axis_index("core")
    meet([(dp, lax.rem(z + step, 4), core) for step in (1, 2, 3)])


def head_lanes(head):
    return pl.ds(pl.multiple_of(head * HD, HD), HD)


def causal_scores(keys, queries, start):
    scores = lax.dot_general(
        keys, queries, (((1,), (1,)), ((), ())), preferred_element_type=jnp.float32
    )
    key_at = lax.broadcasted_iota(jnp.int32, (Q_BLOCK, Q_BLOCK), 0)
    query_at = lax.broadcasted_iota(jnp.int32, (Q_BLOCK, Q_BLOCK), 1)
    edge = jnp.where(key_at <= query_at, scores[start:], MASKED)
    return edge if start == 0 else jnp.concatenate([scores[:start], edge], axis=0)


def attend_kernel(
    exponent, sent, back, held, attended, log_total, mixed, flipped, send, recv, sent_b, recv_b, local
):
    meet_column()
    start, await_arrival, await_sent = column_copies(sent, held, send, recv, local.at[0])
    start_b, await_arrival_b, await_sent_b = column_copies(mixed, back, sent_b, recv_b, local.at[1])
    for block in range(4):
        start(block)
    for block in range(4):
        await_arrival(block)
    chunk = held.shape[1]
    tokens = 4 * chunk
    q_cols = mixed.shape[2]
    for block in range(4):
        flipped[:, chunk * block : chunk * (block + 1)] = held[block, :, q_cols + HD :].T
    per = chunk // Q_BLOCK
    for block in range(tokens // Q_BLOCK):
        first = block * Q_BLOCK
        limit = first + Q_BLOCK

        @pl.loop(0, q_cols // HD)
        def _(head):
            queries = held[block // per, pl.ds((block % per) * Q_BLOCK, Q_BLOCK), head_lanes(head)]
            keys = jnp.concatenate(
                [
                    held[b, : min(chunk, limit - b * chunk), q_cols : q_cols + HD]
                    for b in range(-(-limit // chunk))
                ],
                axis=0,
            )
            scores = causal_scores(keys, queries, first)
            highest = jnp.max(scores, axis=0, keepdims=True)
            weights = jnp.exp2((scores - highest) * exponent)
            total = jnp.sum(weights, axis=0, keepdims=True)
            mix = jnp.dot(
                flipped[:, :limit],
                weights.astype(jnp.bfloat16),
                preferred_element_type=jnp.float32,
            )
            mix = (mix / total).T
            attended[pl.ds(first, Q_BLOCK), head_lanes(head)] = mix
            mixed[block // per, pl.ds((block % per) * Q_BLOCK, Q_BLOCK), head_lanes(head)] = (
                mix.astype(jnp.bfloat16)
            )
            log_total[head, :, pl.ds(first, Q_BLOCK)] = highest * exponent + jnp.log2(total)

        if (block + 1) % per == 0:
            start_b(block // per)
    for block in range(4):
        await_arrival_b(block)
    for block in range(4):
        await_sent(block)
        await_sent_b(block)


def attend_back_kernel(
    exponent,
    sent,
    held,
    attended,
    log_total,
    back,
    landed,
    d_held,
    flipped,
    d_keys,
    d_values,
    send,
    recv,
    sent_b,
    recv_b,
    local,
):
    meet_column()
    start, await_arrival, await_sent = column_copies(sent, landed, send, recv, local.at[0])
    start_b, await_arrival_b, await_sent_b = column_copies(d_held, back, sent_b, recv_b, local.at[1])
    for block in range(4):
        start(block)
    chunk = held.shape[1]
    tokens = 4 * chunk
    q_cols = landed.shape[2]
    for block in range(4):
        flipped[:, chunk * block : chunk * (block + 1)] = held[block, :, q_cols : q_cols + HD].T
    d_keys[...] = jnp.zeros_like(d_keys)
    d_values[...] = jnp.zeros_like(d_values)
    scale = HD ** (-0.5)
    for block in range(4):
        await_arrival(block)
    per = chunk // Q_BLOCK
    for block in reversed(range(tokens // Q_BLOCK)):
        first = block * Q_BLOCK
        limit = first + Q_BLOCK
        rows = pl.ds((block % per) * Q_BLOCK, Q_BLOCK)

        def upto(lanes):
            return jnp.concatenate(
                [
                    held[b, : min(chunk, limit - b * chunk), lanes]
                    for b in range(-(-limit // chunk))
                ],
                axis=0,
            )

        @pl.loop(0, q_cols // HD)
        def _(head):
            queries = held[block // per, rows, head_lanes(head)]
            d_mix = landed[block // per, rows, head_lanes(head)]
            scores = causal_scores(upto(slice(q_cols, q_cols + HD)), queries, first)
            weights = jnp.exp2(scores * exponent - log_total[head, :, pl.ds(first, Q_BLOCK)])
            product = d_mix.astype(jnp.float32) * attended[pl.ds(first, Q_BLOCK), head_lanes(head)]
            row_dot = jnp.sum(product.T, axis=0, keepdims=True)
            d_weights = lax.dot_general(
                upto(slice(q_cols + HD, q_cols + 2 * HD)),
                d_mix,
                (((1,), (1,)), ((), ())),
                preferred_element_type=jnp.float32,
            )
            d_scores = (weights * (d_weights - row_dot)).astype(jnp.bfloat16)
            d_values[:limit] += jnp.dot(
                weights.astype(jnp.bfloat16), d_mix, preferred_element_type=jnp.float32
            )
            d_keys[:limit] += jnp.dot(d_scores, queries, preferred_element_type=jnp.float32)
            d_queries = jnp.dot(flipped[:, :limit], d_scores, preferred_element_type=jnp.float32)
            d_held[block // per, rows, head_lanes(head)] = (d_queries.T * scale).astype(
                jnp.bfloat16
            )

        if block % per == 0:
            part = block // per
            whole = pl.ds(first, chunk)
            d_held[part, :, q_cols : q_cols + HD] = (d_keys[whole] * scale).astype(jnp.bfloat16)
            d_held[part, :, q_cols + HD :] = d_values[whole].astype(jnp.bfloat16)
            start_b(part)
    for block in range(4):
        await_arrival_b(block)
    for block in range(4):
        await_sent(block)
        await_sent_b(block)


EXPONENT = HD ** (-0.5) * math.log2(math.e)
COLUMN_SEMAPHORES = [pltpu.SemaphoreType.DMA((4,))] * 4 + [pltpu.SemaphoreType.DMA((2,))]


def attend_sequence(sent):
    _, chunk, cols = sent.shape
    q_cols = cols - 2 * HD
    return pl.pallas_call(
        functools.partial(attend_kernel, EXPONENT),
        name="attend_sequence",
        out_shape=[
            jax.ShapeDtypeStruct((4, chunk, q_cols), jnp.bfloat16),
            jax.ShapeDtypeStruct((4, chunk, cols), jnp.bfloat16),
            jax.ShapeDtypeStruct((4 * chunk, q_cols), jnp.float32),
            jax.ShapeDtypeStruct((q_cols // HD, 1, 4 * chunk), jnp.float32),
        ],
        in_specs=[HBM],
        out_specs=[HBM, VMEM, VMEM, VMEM],
        scratch_shapes=[
            pltpu.VMEM((4, chunk, q_cols), jnp.bfloat16),
            pltpu.VMEM((HD, 4 * chunk), jnp.bfloat16),
        ]
        + COLUMN_SEMAPHORES,
        compiler_params=pltpu.CompilerParams(
            has_side_effects=True, collective_id=5, vmem_limit_bytes=48 << 20
        ),
        cost_estimate=pl.CostEstimate(flops=0, bytes_accessed=240 << 20, transcendentals=0),
    )(sent)


def attend_sequence_back(sent, held, attended, log_total):
    _, chunk, cols = held.shape
    q_cols = cols - 2 * HD
    return pl.pallas_call(
        functools.partial(attend_back_kernel, EXPONENT),
        name="attend_sequence_back",
        out_shape=jax.ShapeDtypeStruct((4, chunk, cols), jnp.bfloat16),
        in_specs=[HBM, VMEM, VMEM, VMEM],
        out_specs=HBM,
        scratch_shapes=[
            pltpu.VMEM((4, chunk, q_cols), jnp.bfloat16),
            pltpu.VMEM((4, chunk, cols), jnp.bfloat16),
            pltpu.VMEM((HD, 4 * chunk), jnp.bfloat16),
            pltpu.VMEM((4 * chunk, HD), jnp.float32),
            pltpu.VMEM((4 * chunk, HD), jnp.float32),
        ]
        + COLUMN_SEMAPHORES,
        compiler_params=pltpu.CompilerParams(
            has_side_effects=True, collective_id=6, vmem_limit_bytes=48 << 20
        ),
        cost_estimate=pl.CostEstimate(flops=0, bytes_accessed=300 << 20, transcendentals=0),
    )(sent, held, attended, log_total)


def block_scores(queries, keys_all, values_all, first_row, step_index, key_block):
    place = step_index * key_block
    keys_here = lax.dynamic_slice_in_dim(keys_all, place, key_block, 0)
    values_here = lax.dynamic_slice_in_dim(values_all, place, key_block, 0)
    scores = jnp.einsum(
        "tkgd,skd->kgts", queries, keys_here, preferred_element_type=jnp.float32
    ) * queries.shape[-1] ** (-0.5)
    key_rows = place + lax.iota(jnp.int32, key_block)
    query_rows = first_row + lax.iota(jnp.int32, queries.shape[0])
    causal = key_rows[None, :] <= query_rows[:, None]
    return (scores, causal, keys_here, values_here)


def attend(queries, keys_all, values_all, first_row, key_block):
    rows_here = queries.shape[0]
    blocks_needed = (first_row + rows_here + key_block - 1) // key_block
    score_shape = (queries.shape[1], queries.shape[2], rows_here)

    def statistics(step_index, carried):
        running_max, running_sum = carried
        scores, causal, keys_here, values_here = block_scores(
            queries, keys_all, values_all, first_row, step_index, key_block
        )
        scores = jnp.where(causal, scores, MASKED)
        new_max = jnp.maximum(running_max, jnp.max(scores, axis=-1))
        weights_here = jnp.where(causal, jnp.exp(scores - new_max[..., None]), 0.0)
        return (
            new_max,
            running_sum * jnp.exp(running_max - new_max) + jnp.sum(weights_here, axis=-1),
        )

    start_state = (jnp.full(score_shape, MASKED, jnp.float32), jnp.zeros(score_shape, jnp.float32))
    running_max, running_sum = lax.fori_loop(0, blocks_needed, statistics, start_state)
    log_total = running_max + jnp.log(running_sum)

    def weigh(step_index, weighted):
        scores, causal, keys_here, values_here = block_scores(
            queries, keys_all, values_all, first_row, step_index, key_block
        )
        probs = jnp.where(causal, jnp.exp(scores - log_total[..., None]), 0.0).astype(jnp.bfloat16)
        return weighted + jnp.einsum(
            "kgts,skd->tkgd", probs, values_here, preferred_element_type=jnp.float32
        )

    weighted = lax.fori_loop(0, blocks_needed, weigh, jnp.zeros(queries.shape, jnp.float32))
    return (weighted, log_total)


def attend_back(
    queries, keys_all, values_all, first_row, key_block, log_total, d_attended, row_dot
):
    rows_here = queries.shape[0]
    blocks_needed = (first_row + rows_here + key_block - 1) // key_block
    score_scale = queries.shape[-1] ** (-0.5)

    def accumulate(step_index, carried):
        d_queries, d_keys_all, d_values_all = carried
        scores, causal, keys_here, values_here = block_scores(
            queries, keys_all, values_all, first_row, step_index, key_block
        )
        probs = jnp.where(causal, jnp.exp(scores - log_total[..., None]), 0.0)
        d_probs = jnp.einsum(
            "tkgd,skd->kgts", d_attended, values_here, preferred_element_type=jnp.float32
        )
        d_scores = (probs * (d_probs - row_dot[..., None])).astype(jnp.bfloat16)
        d_queries = (
            d_queries
            + jnp.einsum("kgts,skd->tkgd", d_scores, keys_here, preferred_element_type=jnp.float32)
            * score_scale
        )
        d_keys_here = (
            jnp.einsum("kgts,tkgd->skd", d_scores, queries, preferred_element_type=jnp.float32)
            * score_scale
        )
        d_values_here = jnp.einsum(
            "kgts,tkgd->skd",
            probs.astype(jnp.bfloat16),
            d_attended,
            preferred_element_type=jnp.float32,
        )
        place = step_index * key_block
        d_keys_all = lax.dynamic_update_slice_in_dim(d_keys_all, d_keys_here, place, 0)
        d_values_all = lax.dynamic_update_slice_in_dim(d_values_all, d_values_here, place, 0)
        return (d_queries, d_keys_all, d_values_all)

    start_state = (
        jnp.zeros(queries.shape, jnp.float32),
        jnp.zeros(keys_all.shape, jnp.float32),
        jnp.zeros(values_all.shape, jnp.float32),
    )
    return lax.fori_loop(0, blocks_needed, accumulate, start_state)


def weight_gathered(
    inputs,
    targets,
    valid,
    positions,
    ln1_gain,
    w_query,
    w_key,
    w_value,
    w_gatelogit,
    q_gain,
    k_gain,
    w_output,
    ln2_gain,
    w_gate,
    w_up,
    w_down,
):
    attn_full = (
        lax.all_gather(ln1_gain, ("dp", "ctx"), axis=0, tiled=True),
        lax.all_gather(w_query, ("dp", "ctx"), axis=0, tiled=True),
        lax.all_gather(w_key, ("dp", "ctx"), axis=0, tiled=True),
        lax.all_gather(w_value, ("dp", "ctx"), axis=0, tiled=True),
        lax.all_gather(w_gatelogit, ("dp", "ctx"), axis=0, tiled=True),
        lax.all_gather(q_gain, ("dp", "ctx"), axis=0, tiled=True),
        lax.all_gather(k_gain, ("dp", "ctx"), axis=0, tiled=True),
        lax.all_gather(w_output, ("dp", "ctx"), axis=1, tiled=True),
    )
    mlp_full = (
        lax.all_gather(ln2_gain, ("dp", "ctx"), axis=0, tiled=True),
        lax.all_gather(w_gate, ("dp", "ctx"), axis=0, tiled=True),
        lax.all_gather(w_up, ("dp", "ctx"), axis=0, tiled=True),
        lax.all_gather(w_down, ("dp", "ctx"), axis=1, tiled=True),
    )
    gain_one = attn_full[0].astype(jnp.float32)
    gain_q = attn_full[5].astype(jnp.float32)
    gain_k = attn_full[6].astype(jnp.float32)
    gain_two = mlp_full[0].astype(jnp.float32)
    hidden_in = inputs[0].astype(jnp.float32)
    rows_here = hidden_in.shape[0]
    groups = H // KV
    first_row = lax.axis_index("ctx") * rows_here
    cosine, sine = rope_tables(positions[0])
    unit_in = normalize(hidden_in)
    normed_in = (unit_in * gain_one).astype(jnp.bfloat16)
    query_raw = jnp.dot(normed_in, attn_full[1], preferred_element_type=jnp.float32)
    key_raw = jnp.dot(normed_in, attn_full[2], preferred_element_type=jnp.float32)
    value_raw = jnp.dot(normed_in, attn_full[3], preferred_element_type=jnp.float32)
    gate_logit = jnp.dot(normed_in, attn_full[4], preferred_element_type=jnp.float32)
    query_heads = query_raw.reshape(rows_here, H, HD)
    key_heads = key_raw.reshape(rows_here, KV, HD)
    unit_query = normalize(query_heads)
    unit_key = normalize(key_heads)
    queries = (
        apply_rope(unit_query * gain_q, cosine, sine)
        .astype(jnp.bfloat16)
        .reshape(rows_here, KV, groups, HD)
    )
    keys_own = apply_rope(unit_key * gain_k, cosine, sine).astype(jnp.bfloat16)
    values_own = value_raw.reshape(rows_here, KV, HD).astype(jnp.bfloat16)
    keys_all, values_all = (
        lax.all_gather(keys_own, "ctx", axis=0, tiled=True),
        lax.all_gather(values_own, "ctx", axis=0, tiled=True),
    )
    key_block = math.gcd(keys_all.shape[0], 512)
    attended, log_total = attend(queries, keys_all, values_all, first_row, key_block)
    gate_open = jax.nn.sigmoid(gate_logit)
    attended_heads = attended.reshape(rows_here, H, HD)
    gated = (attended_heads * gate_open[:, :, None]).reshape(rows_here, H * HD).astype(jnp.bfloat16)
    middle = hidden_in + jnp.dot(gated, attn_full[7], preferred_element_type=jnp.float32)
    unit_mid = normalize(middle)
    normed_mid = (unit_mid * gain_two).astype(jnp.bfloat16)
    gate_pre = jnp.dot(normed_mid, mlp_full[1], preferred_element_type=jnp.float32)
    up_proj = jnp.dot(normed_mid, mlp_full[2], preferred_element_type=jnp.float32)
    sigmoid_gate = jax.nn.sigmoid(gate_pre)
    activated = (gate_pre * sigmoid_gate * up_proj).astype(jnp.bfloat16)
    result = middle + jnp.dot(activated, mlp_full[3], preferred_element_type=jnp.float32)
    teacher = targets[0].astype(jnp.float32)
    weight_rows = valid[0].astype(jnp.float32)
    difference = result - teacher
    error_local = jnp.sum(weight_rows * jnp.mean(difference * difference, axis=-1))
    error_total, valid_count = lax.psum((error_local, jnp.sum(weight_rows)), ("dp", "ctx"))
    loss = error_total / valid_count
    tokens_all = lax.axis_size("dp") * lax.axis_size("ctx") * rows_here
    d_result = weight_rows[:, None] * difference * (tokens_all / valid_count)
    attn_back = (
        lax.all_gather(ln1_gain, ("dp", "ctx"), axis=0, tiled=True),
        lax.all_gather(w_query, ("dp", "ctx"), axis=0, tiled=True),
        lax.all_gather(w_key, ("dp", "ctx"), axis=0, tiled=True),
        lax.all_gather(w_value, ("dp", "ctx"), axis=0, tiled=True),
        lax.all_gather(w_gatelogit, ("dp", "ctx"), axis=0, tiled=True),
        lax.all_gather(q_gain, ("dp", "ctx"), axis=0, tiled=True),
        lax.all_gather(k_gain, ("dp", "ctx"), axis=0, tiled=True),
        lax.all_gather(w_output, ("dp", "ctx"), axis=1, tiled=True),
    )
    mlp_back = (
        lax.all_gather(ln2_gain, ("dp", "ctx"), axis=0, tiled=True),
        lax.all_gather(w_gate, ("dp", "ctx"), axis=0, tiled=True),
        lax.all_gather(w_up, ("dp", "ctx"), axis=0, tiled=True),
        lax.all_gather(w_down, ("dp", "ctx"), axis=1, tiled=True),
    )
    d_branch = d_result.astype(jnp.bfloat16)
    d_activated = contract_cols(d_branch, mlp_back[3])
    grad_down_full = contract_rows(activated, d_branch)
    d_gate = (
        d_activated * up_proj * sigmoid_gate * (1.0 + gate_pre * (1.0 - sigmoid_gate))
    ).astype(jnp.bfloat16)
    d_up = (d_activated * gate_pre * sigmoid_gate).astype(jnp.bfloat16)
    gate_up_share = lax.psum_scatter(
        jnp.concatenate(
            [contract_rows(normed_mid, d_gate), contract_rows(normed_mid, d_up)], axis=1
        ),
        ("dp", "ctx"),
        scatter_dimension=0,
        tiled=True,
    )
    d_normed_mid = contract_cols(d_gate, mlp_back[1]) + contract_cols(d_up, mlp_back[2])
    grad_gain_two = jnp.sum(d_normed_mid * unit_mid, axis=0)
    d_middle = d_result + norm_back(d_normed_mid * mlp_back[0].astype(jnp.float32), middle)
    d_attn = d_middle.astype(jnp.bfloat16)
    d_gated = contract_cols(d_attn, attn_back[7]).reshape(rows_here, H, HD)
    grad_out_full = contract_rows(gated, d_attn)
    d_attended = (
        (d_gated * gate_open[:, :, None]).astype(jnp.bfloat16).reshape(rows_here, KV, groups, HD)
    )
    d_gate_logit = (
        jnp.sum(d_gated * attended_heads, axis=-1) * gate_open * (1.0 - gate_open)
    ).astype(jnp.bfloat16)
    row_dot = jnp.einsum("tkgd,tkgd->kgt", d_attended.astype(jnp.float32), attended)
    keys_back, values_back = (
        lax.all_gather(keys_own, "ctx", axis=0, tiled=True),
        lax.all_gather(values_own, "ctx", axis=0, tiled=True),
    )
    d_queries, d_keys_all, d_values_all = attend_back(
        queries, keys_back, values_back, first_row, key_block, log_total, d_attended, row_dot
    )
    d_keys, d_values = (
        lax.psum_scatter(
            d_keys_all.astype(jnp.bfloat16), "ctx", scatter_dimension=0, tiled=True
        ).astype(jnp.float32),
        lax.psum_scatter(
            d_values_all.astype(jnp.bfloat16), "ctx", scatter_dimension=0, tiled=True
        ).astype(jnp.float32),
    )
    d_query_rot = rope_back(d_queries.reshape(rows_here, H, HD), cosine, sine)
    grad_gain_q = jnp.sum(d_query_rot * unit_query, axis=(0, 1))
    d_query_raw = (
        norm_back(d_query_rot * attn_back[5].astype(jnp.float32), query_heads)
        .reshape(rows_here, H * HD)
        .astype(jnp.bfloat16)
    )
    d_key_rot = rope_back(d_keys, cosine, sine)
    grad_gain_k = jnp.sum(d_key_rot * unit_key, axis=(0, 1))
    d_key_raw = (
        norm_back(d_key_rot * attn_back[6].astype(jnp.float32), key_heads)
        .reshape(rows_here, KV * HD)
        .astype(jnp.bfloat16)
    )
    d_value_raw = d_values.reshape(rows_here, KV * HD).astype(jnp.bfloat16)
    d_normed_in = contract_cols(d_query_raw, attn_back[1]) + contract_cols(d_key_raw, attn_back[2])
    d_normed_in = (
        d_normed_in
        + contract_cols(d_value_raw, attn_back[3])
        + contract_cols(d_gate_logit, attn_back[4])
    )
    grad_gain_one = jnp.sum(d_normed_in * unit_in, axis=0)
    grad_inputs = d_middle + norm_back(d_normed_in * attn_back[0].astype(jnp.float32), hidden_in)
    grad_query_full = contract_rows(normed_in, d_query_raw)
    grad_key_full = contract_rows(normed_in, d_key_raw)
    grad_value_full = contract_rows(normed_in, d_value_raw)
    grad_logit_full = contract_rows(normed_in, d_gate_logit)
    grad_terms = (
        grad_gain_one,
        grad_query_full,
        grad_key_full,
        grad_value_full,
        grad_logit_full,
        grad_gain_q,
        grad_gain_k,
        grad_out_full,
        grad_gain_two,
        grad_down_full,
    )
    shares = (
        lax.psum_scatter(grad_terms[0], ("dp", "ctx"), scatter_dimension=0, tiled=True),
        lax.psum_scatter(grad_terms[1], ("dp", "ctx"), scatter_dimension=0, tiled=True),
        lax.psum_scatter(grad_terms[2], ("dp", "ctx"), scatter_dimension=0, tiled=True),
        lax.psum_scatter(grad_terms[3], ("dp", "ctx"), scatter_dimension=0, tiled=True),
        lax.psum_scatter(grad_terms[4], ("dp", "ctx"), scatter_dimension=0, tiled=True),
        lax.psum_scatter(grad_terms[5], ("dp", "ctx"), scatter_dimension=0, tiled=True),
        lax.psum_scatter(grad_terms[6], ("dp", "ctx"), scatter_dimension=0, tiled=True),
        lax.psum_scatter(grad_terms[7], ("dp", "ctx"), scatter_dimension=1, tiled=True),
        lax.psum_scatter(grad_terms[8], ("dp", "ctx"), scatter_dimension=0, tiled=True),
        lax.psum_scatter(grad_terms[9], ("dp", "ctx"), scatter_dimension=1, tiled=True),
    )
    ffn_width = w_gate.shape[1]
    return (
        result.astype(jnp.bfloat16)[None],
        loss,
        grad_inputs[None],
        shares[0],
        shares[1],
        shares[2],
        shares[3],
        shares[4],
        shares[5],
        shares[6],
        shares[7],
        shares[8],
        gate_up_share[:, :ffn_width],
        gate_up_share[:, ffn_width:],
        shares[9],
    )


def tensor_parallel(
    dp_n,
    z_n,
    inputs,
    targets,
    valid,
    positions,
    ln1_gain,
    w_query,
    w_key,
    w_value,
    w_gatelogit,
    q_gain,
    k_gain,
    w_output,
    ln2_gain,
    w_gate,
    w_up,
    w_down,
):
    plane_n = dp_n * 2
    rows_here, width = inputs.shape[1:]
    piece = ln1_gain.shape[0]
    group = KV // plane_n
    q_heads = H // plane_n
    q_cols, k_cols = q_heads * HD, group * HD
    ff_cols = w_gate.shape[1] // plane_n
    tokens = plane_n * rows_here
    plane_at = lax.axis_index("dp") * 2 + lax.axis_index("core")

    def to_inner(values):
        lead = values.shape[:-1]
        blocks = values.reshape(lead + (dp_n, z_n, 2 * piece))
        return jnp.swapaxes(blocks, -3, -2).reshape(lead + (width,))

    whole_parts = jnp.concatenate([positions[0], jnp.sum(valid[0])[None].astype(jnp.int32)])
    whole_all = lax.all_gather(whole_parts, EVERY, axis=0).reshape(dp_n, z_n, 2, rows_here + 1)
    valid_count = jnp.sum(whole_all[..., -1]).astype(jnp.float32)
    places = lax.dynamic_index_in_dim(whole_all, lax.axis_index("z"), 1, False)
    places = places[..., :rows_here].reshape(tokens)

    small = jnp.concatenate([ln1_gain, ln2_gain, w_gatelogit.reshape(-1), q_gain, k_gain])
    small_all = lax.all_gather(small, EVERY, axis=0)
    small_inner = jnp.swapaxes(small_all.reshape(dp_n, z_n, 2, -1), 0, 1).reshape(
        small_all.shape
    )
    gain_one = small_inner[:, :piece].reshape(width).astype(jnp.float32)
    gain_two = small_inner[:, piece : 2 * piece].reshape(width).astype(jnp.float32)
    logit_end = 2 * piece + piece * H
    w_logit = small_inner[:, 2 * piece : logit_end].reshape(width, H)
    w_logit = lax.dynamic_slice_in_dim(w_logit, plane_at * q_heads, q_heads, 1)
    head_piece = q_gain.shape[0]
    gain_q = small_all[:, logit_end : logit_end + head_piece].reshape(HD).astype(jnp.float32)
    gain_k = small_all[:, logit_end + head_piece :].reshape(HD).astype(jnp.float32)

    def by_plane(weight):
        return jnp.swapaxes(weight.reshape(piece, plane_n, -1), 0, 1)

    attn_parts = jnp.concatenate(
        [by_plane(w_query), by_plane(w_key), by_plane(w_value), by_plane(w_output.T)], axis=2
    )
    ffn_parts = jnp.concatenate([by_plane(w_gate), by_plane(w_up), by_plane(w_down.T)], axis=2)

    def assemble(parts):
        mine = lax.all_to_all(parts, PLANE, 0, 0, tiled=True)
        mine = mine.reshape(plane_n * piece, parts.shape[2])
        return lax.all_gather(mine, "z", axis=0, tiled=True)

    attn_w = assemble(attn_parts)
    ffn_w = assemble(ffn_parts)
    w_qkv = attn_w[:, : q_cols + 2 * k_cols]
    w_out_t = attn_w[:, q_cols + 2 * k_cols :]
    w_gate_up = ffn_w[:, : 2 * ff_cols]
    w_down_t = ffn_w[:, 2 * ff_cols :]

    hidden_in = to_inner(inputs[0]).astype(jnp.float32)
    unit_in = normalize(hidden_in)
    normed_in = (unit_in * gain_one).astype(jnp.bfloat16)
    normed_all = plane_gather(normed_in)
    cosine, sine = rope_tables(places)
    qkv_raw = matmul(normed_all, w_qkv)
    gate_logit = matmul(normed_all, w_logit)
    query_heads = qkv_raw[:, :q_cols].reshape(tokens, q_heads, HD)
    key_heads = qkv_raw[:, q_cols : q_cols + k_cols].reshape(tokens, group, HD)
    unit_query = normalize(query_heads)
    unit_key = normalize(key_heads)
    queries = apply_rope(unit_query * gain_q, cosine, sine).astype(jnp.bfloat16)
    keys = apply_rope(unit_key * gain_k, cosine, sine).astype(jnp.bfloat16)
    sent = jnp.concatenate(
        [
            queries.reshape(tokens, q_cols),
            keys.reshape(tokens, k_cols),
            qkv_raw[:, q_cols + k_cols :].astype(jnp.bfloat16),
        ],
        axis=1,
    )
    attended_back, held, attended, log_total = attend_sequence(sent.reshape(dp_n, -1, sent.shape[1]))
    attended_heads = attended_back.reshape(tokens, q_heads, HD).astype(jnp.float32)
    gate_open = jax.nn.sigmoid(gate_logit)
    gated = (attended_heads * gate_open[:, :, None]).reshape(tokens, q_cols).astype(jnp.bfloat16)
    partial = contract_cols(gated, w_out_t).astype(jnp.bfloat16)
    middle, normed_mid = plane_sum(
        "middle_sum",
        1,
        middle_tail,
        partial,
        (inputs[0], gain_two[None]),
        [((rows_here, width), jnp.float32)],
        True,
    )
    gate_up = matmul(normed_mid, w_gate_up)
    gate_pre, up_proj = gate_up[:, :ff_cols], gate_up[:, ff_cols:]
    sigmoid_gate = jax.nn.sigmoid(gate_pre)
    activated = (gate_pre * sigmoid_gate * up_proj).astype(jnp.bfloat16)
    partial = contract_cols(activated, w_down_t).astype(jnp.bfloat16)
    counted = valid[0].astype(jnp.float32)[:, None]
    tokens_all = dp_n * z_n * 2 * rows_here
    result, d_result, error_sums, d_branch = plane_sum(
        "result_sum",
        2,
        result_tail,
        partial,
        (middle, targets[0], counted, counted * (tokens_all / valid_count)),
        [
            ((rows_here, width), jnp.bfloat16),
            ((rows_here, width), jnp.float32),
            ((STRIP, width), jnp.float32),
        ],
        True,
    )
    error_local = jnp.sum(error_sums) / width
    d_activated = matmul(d_branch, w_down_t)
    grad_down_t = contract_rows(d_branch, activated).astype(jnp.bfloat16)
    d_gate = d_activated * up_proj * sigmoid_gate * (1.0 + gate_pre * (1.0 - sigmoid_gate))
    d_up = d_activated * gate_pre * sigmoid_gate
    d_gate_up = jnp.concatenate([d_gate, d_up], axis=1).astype(jnp.bfloat16)
    grad_gate_up = contract_rows(normed_mid, d_gate_up).astype(jnp.bfloat16)
    partial = contract_cols(d_gate_up, w_gate_up).astype(jnp.bfloat16)
    d_middle, gain_two_sums, d_attn = plane_sum(
        "middle_back_sum",
        3,
        middle_back_tail,
        partial,
        (middle, gain_two[None], d_result),
        [((rows_here, width), jnp.float32), ((STRIP, width), jnp.float32)],
        True,
    )
    grad_gain_two = jnp.sum(gain_two_sums, axis=0)

    def settle(grads):
        summed = lax.psum_scatter(grads, "z", scatter_dimension=0, tiled=True)
        return lax.all_to_all(
            summed.reshape(plane_n, piece, grads.shape[1]), PLANE, 0, 0, tiled=True
        )

    def take(settled, start, size):
        part = jnp.swapaxes(settled[:, :, start : start + size], 0, 1)
        return part.reshape(piece, plane_n * size).astype(jnp.float32)

    gate_up_own = settle(grad_gate_up)
    down_own = settle(grad_down_t)

    d_gated = matmul(d_attn, w_out_t).reshape(tokens, q_heads, HD)
    grad_out_t = contract_rows(d_attn, gated).astype(jnp.bfloat16)
    d_attended = (d_gated * gate_open[:, :, None]).astype(jnp.bfloat16)
    d_gate_logit = (
        jnp.sum(d_gated * attended_heads, axis=-1) * gate_open * (1.0 - gate_open)
    ).astype(jnp.bfloat16)
    held = attend_sequence_back(
        d_attended.reshape(dp_n, -1, q_cols), held, attended, log_total
    ).reshape(tokens, -1)
    d_query_rot = rope_back(
        held[:, :q_cols].reshape(tokens, q_heads, HD).astype(jnp.float32), cosine, sine
    )
    d_key_rot = rope_back(
        held[:, q_cols : q_cols + k_cols].reshape(tokens, group, HD).astype(jnp.float32),
        cosine,
        sine,
    )
    grad_gain_q = jnp.sum(d_query_rot * unit_query, axis=(0, 1))
    grad_gain_k = jnp.sum(d_key_rot * unit_key, axis=(0, 1))
    d_qkv = jnp.concatenate(
        [
            norm_back(d_query_rot * gain_q, query_heads)
            .reshape(tokens, q_cols)
            .astype(jnp.bfloat16),
            norm_back(d_key_rot * gain_k, key_heads).reshape(tokens, k_cols).astype(jnp.bfloat16),
            held[:, q_cols + k_cols :],
        ],
        axis=1,
    )
    grad_qkv = contract_rows(normed_all, d_qkv).astype(jnp.bfloat16)
    grad_logit = contract_rows(normed_all, d_gate_logit)
    attn_own = settle(jnp.concatenate([grad_qkv, grad_out_t], axis=1))
    d_normed_in = contract_cols(d_qkv, w_qkv) + contract_cols(d_gate_logit, w_logit)
    grad_inputs, gain_one_sums = plane_sum(
        "inputs_back_sum",
        4,
        inputs_back_tail,
        d_normed_in.astype(jnp.bfloat16),
        (inputs[0], gain_one[None], d_middle),
        [((rows_here, width), jnp.float32), ((STRIP, width), jnp.float32)],
        False,
    )
    grad_gain_one = jnp.sum(gain_one_sums, axis=0)

    devices = dp_n * z_n * 2
    logit_wide = lax.dynamic_update_slice(
        jnp.zeros((width, H), jnp.float32), grad_logit, (0, plane_at * q_heads)
    )

    def outer_rows(values):
        return jnp.swapaxes(values.reshape(z_n, dp_n, 2, -1), 0, 1).reshape(devices, -1)

    small_sums = jnp.concatenate(
        [
            outer_rows(grad_gain_one),
            outer_rows(grad_gain_two),
            outer_rows(logit_wide),
            grad_gain_q.reshape(devices, -1),
            grad_gain_k.reshape(devices, -1),
            jnp.full((devices, 1), error_local),
        ],
        axis=1,
    )
    small_own = lax.psum_scatter(small_sums.reshape(-1), EVERY, scatter_dimension=0, tiled=True)
    loss = small_own[-1] / valid_count
    return (
        result[None],
        loss,
        grad_inputs[None],
        small_own[:piece],
        take(attn_own, 0, q_cols),
        take(attn_own, q_cols, k_cols),
        take(attn_own, q_cols + k_cols, k_cols),
        small_own[2 * piece : logit_end].reshape(piece, H),
        small_own[logit_end : logit_end + head_piece],
        small_own[logit_end + head_piece : -1],
        take(attn_own, q_cols + 2 * k_cols, q_cols).T,
        small_own[piece : 2 * piece],
        take(gate_up_own, 0, ff_cols),
        take(gate_up_own, ff_cols, ff_cols),
        take(down_own, 0, ff_cols).T,
    )


def solution(mesh):
    dp_n, ctx_n = mesh.shape["dp"], mesh.shape["ctx"]
    split = dp_n == 4 and ctx_n == 8
    if split:
        mesh = Mesh(mesh.devices.reshape(dp_n, ctx_n // 2, 2), EVERY)
        on_device = functools.partial(tensor_parallel, dp_n, ctx_n // 2)
        ctx, every = ("z", "core"), EVERY
    else:
        on_device = weight_gathered
        ctx, every = "ctx", ("dp", "ctx")
    tokens, rows, cols, flat = P("dp", ctx, None), P(every, None), P(None, every), P(every)
    return jax.shard_map(
        on_device,
        mesh=mesh,
        in_specs=(
            tokens,
            tokens,
            P("dp", ctx),
            P("dp", ctx),
            flat,
            rows,
            rows,
            rows,
            rows,
            flat,
            flat,
            cols,
            flat,
            rows,
            rows,
            cols,
        ),
        out_specs=(
            tokens,
            P(),
            tokens,
            flat,
            rows,
            rows,
            rows,
            rows,
            flat,
            flat,
            cols,
            flat,
            rows,
            rows,
            cols,
        ),
        check_vma=False,
    )
```
